128 devices in a mesh: rows: 32 (over x, y, core), eig: 4 (over z).
Axes of the slice: x: 4, y: 4, z: 4, core: 2. Of those that a mesh axis runs over, the one named last changes fastest.
Arguments:
- phi_obs: bfloat16 [16384, 4096], P('rows', 'eig'), may hold values from -0.09375 to 0.09375
- counts: int32 [32], P('rows'), may hold values from 1 to 512, as said below
- targets: bfloat16 [16384, 128], P('rows', 'eig'), may hold values from -6 to 6
- spectrum: float32 [4096], replicated, may hold values from 0.1 to 10
- coef_noise: float32 [4096, 128], replicated, may hold values from -6 to 6
- phi_slab: bfloat16 [65536, 4096], P('rows', 'eig'), may hold values from -0.09375 to 0.09375
Outputs:
- factor: float32 [4096, 4096], P('rows', 'eig')
- solved: float32 [4096, 128], P('rows', 'eig')
- slab_prior: float32 [65536, 128], P(('rows', 'eig'))
The draws below stay inside these ranges and needn't reach their ends.
Inputs may be any that keep to these rules, and one draw needn't show every extreme that they name: counts[r] is the number of live rows of shard r, which come first in the shard; some shard is full (512).
All inputs are finite; a program needn't handle non-finite values.
Results may differ from the reference program's by a relative error of at most 0.0029.
Values may be sent and summed in bfloat16 or wider, within the bound.
No kernel may reach another device: no remote copies, remote signals or barrier semaphores. Data moves between devices by JAX's collectives and lax.ppermute only.
A program may use at most 192 MiB of HBM per device.

```python
import math
import jax
import jax.numpy as jnp
from jax import lax

M = 4096
PANEL = 512
SAMPLES = 128
OBS_DEV = 512
SHARDS = 32
OBS = 16384
SLAB = 65536
N_ROWS = 32


def draw_counts(key, part):
    first_key, second_key, third_key = jax.random.split(key, 3)
    first = jax.random.randint(first_key, (SHARDS,), 1, OBS_DEV + 1)
    second = jax.random.randint(second_key, (SHARDS,), 1, OBS_DEV + 1)
    base = jnp.maximum(1, first * second // OBS_DEV)
    chosen = jax.random.randint(third_key, (), 0, SHARDS)
    return jnp.where(jnp.arange(SHARDS) == chosen, OBS_DEV, base).astype(jnp.int32)


def shard_levels(own_key, dims, pieces, low, top_value):
    factor_of = 1.0
    for axis_at, parts in pieces:
        draws = jax.random.uniform(jax.random.fold_in(jax.random.fold_in(own_key, 6), axis_at), (parts,), jnp.float32, low / len(pieces), top_value / len(pieces))
        factor_of = factor_of * jnp.repeat(jnp.exp(draws), dims[axis_at] // parts).reshape((-1,) + (1,) * (len(dims) - 1 - axis_at))
    return factor_of


def scatter_about(key, shape, scale, bound, pieces=(), held_as=jnp.bfloat16):
    values = scale * jax.random.normal(key, shape, jnp.float32)
    if pieces:
        values = values * shard_levels(key, shape, pieces, -0.22, 0.18)
    return jnp.clip(values, -bound, bound).astype(held_as)


def setup_inputs(seed: int = 0) -> dict:
    seeds = jax.random.split(jax.random.key(seed), 7)
    phi_obs = scatter_about(seeds[0], (OBS, M), (OBS_DEV * N_ROWS // 4) ** -0.5, 0.09375, ((0, 32), (1, 4)))
    counts = draw_counts(jax.random.fold_in(seeds[6], 71), 0)
    targets = scatter_about(seeds[2], (OBS, SAMPLES), 1.0, 6.0, ((0, 32), (1, 4)))
    spectrum = jnp.clip(jnp.exp(jax.random.uniform(seeds[3], (M,), jnp.float32, math.log(0.1), math.log(10.0))), 0.1, 10.0)
    coef_noise = scatter_about(seeds[4], (M, SAMPLES), 1.0, 6.0, (), jnp.float32)
    phi_slab = scatter_about(seeds[5], (SLAB, M), M ** -0.5, 0.09375, ((0, 32), (1, 4)))
    return dict(phi_obs=phi_obs, counts=counts, targets=targets, spectrum=spectrum, coef_noise=coef_noise, phi_slab=phi_slab)


def reference(phi_obs, counts, targets, spectrum, coef_noise, phi_slab):
    shards = counts.shape[0]
    rows_each = phi_obs.shape[0] // shards
    position = jnp.arange(rows_each, dtype=jnp.int32)
    keep = (position[None, :] < counts[:, None]).reshape(-1)
    live = jnp.where(keep[:, None], phi_obs, jnp.zeros_like(phi_obs))
    live_targets = jnp.where(keep[:, None], targets, jnp.zeros_like(targets))
    gram = jnp.dot(live.T.astype(jnp.float32), live.astype(jnp.float32), preferred_element_type=jnp.float32)
    order = gram.shape[0]
    precision = gram + jnp.diag(1.0 / spectrum)
    head = jnp.linalg.cholesky(precision[:PANEL, :PANEL])
    lower = jax.scipy.linalg.solve_triangular(head, precision[PANEL:, :PANEL].T, lower=True).T
    trailing = precision[PANEL:, PANEL:] - jnp.dot(lower, lower.T, precision=lax.Precision.HIGHEST)
    top = jnp.concatenate([head, jnp.zeros((PANEL, order - PANEL), jnp.float32)], axis=1)
    bottom = jnp.concatenate([lower, trailing], axis=1)
    factor = jnp.concatenate([top, bottom], axis=0)
    rhs = jnp.dot(live.T.astype(jnp.float32), live_targets.astype(jnp.float32), preferred_element_type=jnp.float32)
    rhs = rhs + coef_noise / jnp.sqrt(spectrum)[:, None]
    first = jax.scipy.linalg.solve_triangular(head, rhs[:PANEL], lower=True)
    rest = rhs[PANEL:] - jnp.dot(lower, first, precision=lax.Precision.HIGHEST)
    solved = jnp.concatenate([first, rest], axis=0)
    scaled = (jnp.sqrt(spectrum)[:, None] * coef_noise).astype(jnp.bfloat16)
    slab_prior = jnp.dot(phi_slab.astype(jnp.float32), scaled.astype(jnp.float32), preferred_element_type=jnp.float32)
    return (factor, solved, slab_prior)
```

```python
import jax
import jax.numpy as jnp
from jax import lax
from jax.sharding import PartitionSpec as P

PANEL = 512
BLOCK = 128
EXACT = lax.Precision.HIGHEST


def contract_rows(left, right):
    return lax.dot_general(
        left, right, (((0,), (0,)), ((), ())), preferred_element_type=jnp.float32
    )


def mul(left, right):
    return jnp.dot(left, right, precision=EXACT)


def factor_head(head_matrix):
    steps = PANEL // BLOCK
    eye = jnp.eye(BLOCK, dtype=jnp.float32)
    remaining = head_matrix
    columns = []
    inverse_rows = []
    for step in range(steps):
        diagonal = jnp.linalg.cholesky(remaining[:BLOCK, :BLOCK], symmetrize_input=False)
        inverse = jax.scipy.linalg.solve_triangular(diagonal, eye, lower=True)
        column = diagonal
        if step + 1 < steps:
            below = mul(remaining[BLOCK:, :BLOCK], inverse.T)
            remaining = remaining[BLOCK:, BLOCK:] - mul(below, below.T)
            column = jnp.concatenate([diagonal, below], axis=0)
        columns.append(column)
        row = inverse
        if step:
            left = jnp.concatenate(
                [
                    columns[c][(step - c) * BLOCK : (step - c + 1) * BLOCK]
                    for c in range(step)
                ],
                axis=1,
            )
            above = jnp.concatenate(
                [jnp.pad(r, ((0, 0), (0, step * BLOCK - r.shape[1]))) for r in inverse_rows],
                axis=0,
            )
            row = jnp.concatenate([-mul(mul(inverse, left), above), inverse], axis=1)
        inverse_rows.append(row)
    head = jnp.concatenate(
        [jnp.pad(c, ((PANEL - c.shape[0], 0), (0, 0))) for c in columns], axis=1
    )
    head_inverse = jnp.concatenate(
        [jnp.pad(r, ((0, 0), (0, PANEL - r.shape[1]))) for r in inverse_rows], axis=0
    )
    return head, head_inverse


def on_device(phi_obs, counts, targets, spectrum, coef_noise, phi_slab):
    rows_total = lax.axis_size("rows")
    eig_total = lax.axis_size("eig")
    row_index = lax.axis_index("rows")
    eig_index = lax.axis_index("eig")
    obs_slots, width_dev = phi_obs.shape
    order = width_dev * eig_total
    row_share = order // rows_total
    rows_per_eig = rows_total // eig_total
    sample_share = targets.shape[1]
    slab_share = phi_slab.shape[0] // eig_total
    position = jnp.arange(obs_slots, dtype=jnp.int32)
    keep = (position < counts[0])[:, None]
    local_rows = jnp.where(keep, phi_obs, jnp.zeros_like(phi_obs))
    local_targets = jnp.where(keep, targets, jnp.zeros_like(targets))
    full_rows = lax.all_gather(local_rows, "eig", axis=1, tiled=True)

    spectrum_block = lax.dynamic_slice_in_dim(spectrum, eig_index * width_dev, width_dev, 0)
    noise_block = lax.dynamic_slice_in_dim(coef_noise, eig_index * width_dev, width_dev, 0)
    scaled = (jnp.sqrt(spectrum_block)[:, None] * noise_block).astype(jnp.bfloat16)
    slab_part = jnp.dot(phi_slab, scaled, preferred_element_type=jnp.float32)

    def slab_piece(owner):
        return lax.dynamic_slice_in_dim(slab_part, owner * slab_share, slab_share, 0)

    slab_prior = slab_piece(eig_index)
    for shift in range(1, eig_total):
        ring = [(e, (e + shift) % eig_total) for e in range(eig_total)]
        owner = (eig_index + shift) % eig_total
        slab_prior = slab_prior + lax.ppermute(slab_piece(owner), "eig", ring)

    panel_cols = full_rows[:, :PANEL]
    head_part = contract_rows(panel_cols, panel_cols)
    rhs_part = contract_rows(local_targets, full_rows)
    head_gram, rhs_data = lax.psum((head_part, rhs_part), "rows")
    panel_part = contract_rows(panel_cols, local_rows)
    panel_piece = lax.psum_scatter(panel_part, "rows", scatter_dimension=0, tiled=True)
    panel_gram = lax.all_gather(panel_piece, "rows", axis=0, tiled=True)
    gram_part = contract_rows(full_rows, local_rows)
    gram_block = lax.psum_scatter(gram_part, "rows", scatter_dimension=0, tiled=True)

    inverse_prior = 1.0 / spectrum
    col_ids = eig_index * width_dev + jnp.arange(width_dev, dtype=jnp.int32)
    row_ids = row_index * row_share + jnp.arange(row_share, dtype=jnp.int32)
    panel_ids = jnp.arange(PANEL, dtype=jnp.int32)
    zero = jnp.float32(0.0)
    prior_head = inverse_prior[:PANEL, None]
    head_matrix = head_gram + jnp.where(
        panel_ids[:, None] == panel_ids[None, :], prior_head, zero
    )
    panel = panel_gram + jnp.where(panel_ids[:, None] == col_ids[None, :], prior_head, zero)

    own_piece = lax.dynamic_slice_in_dim(
        panel, (row_index % rows_per_eig) * row_share, row_share, 1
    )
    row_panel = jnp.where(eig_index == row_index // rows_per_eig, own_piece, zero)
    for shift in range(1, eig_total):
        pairs = []
        for r in range(rows_total):
            source = r // rows_per_eig
            target = (source + shift) % eig_total
            pairs.append((r * eig_total + source, r * eig_total + target))
        row_panel = row_panel + lax.ppermute(own_piece, ("rows", "eig"), pairs)

    head, head_inverse = factor_head(head_matrix)
    solved_cols = mul(head_inverse, panel)
    solved_rows = mul(head_inverse, row_panel)
    noise_cols = lax.dynamic_slice_in_dim(coef_noise, eig_index * sample_share, sample_share, 1)
    rhs_all = rhs_data + (noise_cols / jnp.sqrt(spectrum)[:, None]).T
    first = mul(rhs_all[:, :PANEL], head_inverse.T)
    in_head = row_index * row_share < PANEL
    head_start = jnp.minimum(row_index * row_share, PANEL - row_share)
    head_rows = lax.dynamic_slice_in_dim(head, head_start, row_share, 0)
    first_rows = lax.dynamic_slice_in_dim(first, head_start, row_share, 1)
    my_rhs = lax.dynamic_slice_in_dim(rhs_all, row_index * row_share, row_share, 1)
    solved = jnp.where(in_head, first_rows, my_rhs - mul(first, solved_rows)).T
    my_factor_rows = jnp.where(in_head, head_rows, solved_rows.T)
    update = mul(solved_rows.T, solved_cols)
    my_prior = lax.dynamic_slice_in_dim(inverse_prior, row_index * row_share, row_share, 0)
    on_diagonal = row_ids[:, None] == col_ids[None, :]
    schur = gram_block + jnp.where(on_diagonal, my_prior[:, None], zero) - update
    panel_out = jnp.pad(my_factor_rows, ((0, 0), (0, width_dev - PANEL)))
    trailing = jnp.where(in_head, zero, schur)
    factor = jnp.where(col_ids[None, :] < PANEL, panel_out, trailing)
    return (factor, solved, slab_prior)


def solution(mesh):
    return jax.shard_map(
        on_device,
        mesh=mesh,
        in_specs=(P("rows", "eig"), P("rows"), P("rows", "eig"), P(), P(), P("rows", "eig")),
        out_specs=(P("rows", "eig"), P("rows", "eig"), P(("rows", "eig"), None)),
        check_vma=False,
    )
```
